256 devices in a mesh: enc: 16 (over z, core), vocab: 8 (over x, y_hi), grp: 2 (over y_lo).
Axes of the slice: x: 4, y: 4 (y_hi: 2, y_lo: 2; y = y_hi * 2 + y_lo), z: 8, core: 2. Of those that a mesh axis runs over, the one named last changes fastest.
Arguments:
- hidden: bfloat16 [12288, 1024], P('enc', ('vocab', 'grp')), may hold values from -6 to 6
- dense_weight: bfloat16 [1024, 1024], P('enc'), may hold values from -0.1875 to 0.1875
- head_weight: bfloat16 [1024, 126976], P('enc', ('vocab', 'grp')), may hold values from -0.1875 to 0.1875
- head_bias: float32 [126976], P(('vocab', 'grp')), may hold values from -4 to 4
- lengths: int32 [48], P('enc'), may hold values from 64 to 256, as said below
- queries: bfloat16 [128, 126976], P('enc', ('vocab', 'grp')), may hold values from -0.25 to 0.25283518
- positives: int32 [128], replicated, may hold values from 0 to 47
Outputs:
- batch_loss: float32 [], replicated
- query_grad: float32 [128, 126976], P('enc', ('vocab', 'grp'))
- passage_grad: float32 [48, 126976], P('enc', ('vocab', 'grp'))
The draws below stay inside these ranges and needn't reach their ends.
Inputs may be any that keep to these rules, and one draw needn't show every extreme that they name: `lengths`: each 3 passages in a row hold, among their first two, one with 256 valid tokens and one with 64.
All inputs are finite; a program needn't handle non-finite values.
Results may differ from the reference program's by a relative error of at most 0.035.
Values may be sent and summed in bfloat16 or wider, within the bound.
A program may use at most 128 MiB of HBM per device.

```python
import jax
import jax.numpy as jnp
from jax import lax

D = 1024
SEQ = 256
PASS_DEV = 3
NP = 48
NQ = 128
TOKENS = 12288
VOCAB = 126976


def draw_queries(key, part):
    noise_key = jax.random.fold_in(jax.random.fold_in(key, 11), 0)
    values = 0.03 * jax.random.normal(noise_key, (NQ, VOCAB), jnp.float32)
    values = jnp.clip(values, -0.25, 0.25)
    return values.astype(jnp.bfloat16)


def draw_lengths(key, part):
    picks = jax.random.randint(jax.random.fold_in(key, 23), (NP,), SEQ // 4, SEQ + 1)
    flips = jax.random.randint(jax.random.fold_in(key, 29), (NP // PASS_DEV,), 0, 2)
    flip_rows = jnp.repeat(flips, PASS_DEV)
    within = jnp.arange(NP) % PASS_DEV
    first_len = jnp.where(flip_rows == 1, SEQ // 4, SEQ)
    second_len = jnp.where(flip_rows == 1, SEQ, SEQ // 4)
    picks = jnp.where(within == 0, first_len, picks)
    return jnp.where(within == 1, second_len, picks).astype(jnp.int32)


def draw_positives(key, part):
    picks = jax.random.randint(jax.random.fold_in(key, 37), (NQ,), 0, NP)
    slots = jnp.arange(NQ)
    picks = jnp.where(slots == 0, NP - 1, picks)
    return jnp.where(slots == 1, 0, picks).astype(jnp.int32)


def block_scale(stream_key, shape, cuts, low, largest):
    loudness = 1.0
    for axis_at, blocks in cuts:
        steps = jax.random.uniform(jax.random.fold_in(jax.random.fold_in(stream_key, 6), axis_at), (blocks,), jnp.float32, low / len(cuts), largest / len(cuts))
        loudness = loudness * jnp.repeat(jnp.exp(steps), shape[axis_at] // blocks).reshape((-1,) + (1,) * (len(shape) - 1 - axis_at))
    return loudness


def normal_values(own_key, extent, deviation, bound, cuts=(), kind=jnp.bfloat16):
    factor_of = block_scale(own_key, extent, cuts, -0.22, 0.18) if cuts else 1.0
    drawn = jax.random.normal(own_key, extent, jnp.float32) * deviation * factor_of
    return jnp.minimum(jnp.maximum(drawn, -bound), bound).astype(kind)


def setup_inputs(seed: int = 0) -> dict:
    seeds = jax.random.split(jax.random.key(seed), 8)
    return {
        "hidden": normal_values(seeds[0], (TOKENS, D), 1.0, 6.0, ((0, 16), (1, 16))),
        "dense_weight": normal_values(seeds[1], (D, D), D ** -0.5, 0.1875, ((0, 16),)),
        "head_weight": normal_values(seeds[2], (D, VOCAB), D ** -0.5, 0.1875, ((0, 16), (1, 16))),
        "head_bias": normal_values(seeds[3], (VOCAB,), 1.0, 4.0, ((0, 16),), jnp.float32),
        "lengths": draw_lengths(jax.random.fold_in(seeds[7], 71), 0),
        "queries": draw_queries(jax.random.fold_in(seeds[7], 71), 0),
        "positives": draw_positives(jax.random.fold_in(seeds[7], 71), 0),
    }


def transform_rows(hidden, dense_weight):
    pre_act = jnp.dot(hidden, dense_weight, preferred_element_type=jnp.float32)
    activated = jax.nn.gelu(pre_act, approximate=False)
    center = lax.optimization_barrier(jnp.mean(activated, axis=-1, keepdims=True))
    spread = lax.optimization_barrier(jnp.mean(jnp.square(activated - center), axis=-1, keepdims=True))
    return ((activated - center) * lax.rsqrt(spread + 1e-05)).astype(jnp.bfloat16)

def softmax_grads(scores, chosen):
    peak_val = lax.optimization_barrier(jnp.max(scores, axis=1, keepdims=True))
    log_total = jnp.log(lax.optimization_barrier(jnp.sum(jnp.exp(scores - peak_val), axis=1, keepdims=True))) + peak_val
    columns = lax.broadcasted_iota(jnp.int32, scores.shape, 1)
    is_positive = columns == chosen.astype(jnp.int32)[:, None]
    picked_score = lax.optimization_barrier(jnp.sum(jnp.where(is_positive, scores, jnp.zeros_like(scores)), axis=1))
    batch_loss = jnp.sum(log_total[:, 0] - picked_score)
    score_grad = (jnp.exp(scores - log_total) - is_positive.astype(scores.dtype)).astype(jnp.bfloat16)
    return (batch_loss, score_grad)

def reference(hidden, dense_weight, head_weight, head_bias, lengths, queries, positives):
    normed = transform_rows(hidden, dense_weight)
    passages = lengths.shape[0]
    by_passage = normed.reshape(passages, SEQ, normed.shape[1])
    positions = jnp.arange(SEQ, dtype=jnp.int32)

    def per_passage(inputs):
        token_rows, token_count = inputs
        logits = jnp.dot(token_rows, head_weight, preferred_element_type=jnp.float32) + head_bias
        is_valid = (positions < token_count)[:, None]
        masked = jnp.where(is_valid, logits, jnp.full_like(logits, -jnp.inf))
        peak_val = lax.optimization_barrier(jnp.max(masked, axis=0))
        return jnp.log1p(jnp.maximum(peak_val, 0.0)).astype(jnp.bfloat16)
    pass_reps = lax.map(per_passage, (by_passage, lengths))
    scores = jnp.dot(queries, pass_reps.T, preferred_element_type=jnp.float32)
    loss_sum, score_grad = softmax_grads(scores, positives)
    batch_loss = loss_sum / scores.shape[0]
    query_grad = jnp.dot(score_grad, pass_reps, preferred_element_type=jnp.float32)
    passage_grad = jnp.dot(score_grad.T, queries, preferred_element_type=jnp.float32)
    return (batch_loss, query_grad, passage_grad)
```

```python
import jax
import jax.numpy as jnp
import numpy as np
from jax import lax
from jax.experimental import pallas as pl
from jax.experimental.pallas import tpu as pltpu
from jax.sharding import PartitionSpec as P

NX, NY, NZ = 4, 4, 8
NE, NV = 16, 16
D = 1024
FW = D // NY
COLS = 7936
CW = 512
BIG, SHORT = 128, 32
ROWS = BIG + SHORT
NQ = 128
REPS = 48
HALF = REPS // 2
MESH = pl.DeviceIdType.MESH
F32, BF16 = jnp.float32, jnp.bfloat16
AWAY = (1, 15, 2, 14, 3, 13, 4, 12, 5, 11, 6, 10, 7, 9, 8)


def place():
    enc, vocab, grp = lax.axis_index("enc"), lax.axis_index("vocab"), lax.axis_index("grp")
    return enc // 2, enc % 2, vocab // 2, (vocab % 2) * 2 + grp


def device(z, c, x, y):
    return (2 * z + c, 2 * x + y // 2, y % 2)


def first_col(enc):
    return pl.multiple_of(jnp.minimum(CW * enc, COLS - CW), 128)


def aligned(start, size):
    return pl.ds(pl.multiple_of(start, size), size)


def arrived(ref, sem):
    pltpu.make_async_copy(ref, ref, sem).wait()


def send(src, dst, send_sem, recv_sem, to):
    pltpu.make_async_remote_copy(
        src_ref=src, dst_ref=dst, send_sem=send_sem, recv_sem=recv_sem,
        device_id=to, device_id_type=MESH,
    ).start()


def ring_order(z):
    return [(z + off + NZ) % NZ for off in (0, -1, 1, -2, 2, -3, 3, -4)]


def kernel(
    lens, hid, dense, weight, queries, bias, positives, loss, query_out, pass_out,
    hidv, hsel, hrecv, xrows, dn, act, stat, stat_all, tb, wx, pool, mx, qall, qfull, rfull,
    biasv, sp, cbuf, xbuf, ybuf, zbuf, fin, gradT,
    loc, h_s, h_r, d_s, d_r, ds_s, w_s, w_r, q_s, q_r, st_s, st_r,
    tz_s, ty_s, t_r, ts_s, ts_r, wx_s, wx_r, g_s, g_r, gs_s, p_s, p_r,
    r_s, r_r, rs_s, c_s, c_r, x_s, x_r, y_s, y_r, z_s, z_r,
):
    z, c, x, y = place()
    enc, v = 2 * z + c, 4 * x + y
    zs = ring_order(z)
    up, down = device((z + 1) % NZ, c, x, y), device((z + NZ - 1) % NZ, c, x, y)
    sibling = device(z, 1 - c, x, y)
    xr, xl, xo = (x + 1) % NX, (x + 3) % NX, (x + 2) % NX
    yr, yl, yo = (y + 1) % NY, (y + 3) % NY, (y + 2) % NY
    features = aligned(FW * y, FW)

    def dense_rows(zz, cc):
        return dn.at[aligned(64 * (2 * zz + cc), 64), :]

    def w_rows(xx, ee):
        return wx.at[xx, aligned(64 * ee, 64), :]

    def w_pair(xx, zz):
        return wx.at[xx, aligned(128 * zz, 128), :]

    def q_part(ee):
        return qall.at[aligned(8 * ee, 8), :]

    def q_rows(zz, cc):
        return qfull.at[aligned(8 * (2 * zz + cc), 8), :]

    own_hid = pltpu.make_async_copy(hid, hidv, loc.at[0])
    own_hid.start()
    own_cols = pl.ds(first_col(enc), CW)
    own_dense = pltpu.make_async_copy(dense.at[:, features], dense_rows(z, c), loc.at[1])
    own_w = pltpu.make_async_copy(weight.at[:, own_cols], w_rows(x, enc), loc.at[2])
    own_q = pltpu.make_async_copy(queries.at[:, own_cols], q_part(enc), loc.at[3])
    own_rows = pltpu.make_async_copy(queries, q_rows(z, c), loc.at[4])
    own_bias = pltpu.make_async_copy(bias.at[:, own_cols], biasv, loc.at[5])
    for copy in (own_dense, own_w, own_q, own_rows, own_bias):
        copy.start()

    bar = pltpu.get_barrier_semaphore()
    for i in range(1, NE):
        to = (enc + i) % NE
        pl.semaphore_signal(
            bar, inc=1, device_id=device(to // 2, to % 2, x, y), device_id_type=MESH
        )
    for i in range(1, 2 * NV):
        if i != NV:
            at = (16 * c + v + i) % 32
            pl.semaphore_signal(
                bar, inc=1, device_id=device(z, at // 16, (at // 4) % 4, at % 4),
                device_id_type=MESH,
            )

    own_hid.wait()
    n_first, n_third = lens[0], lens[2]
    swapped = jnp.full((64, 256), n_first, jnp.int32) < 256
    first, second = hidv[:, 0:256].astype(F32), hidv[:, 256:512].astype(F32)
    third = hidv[:, 512:768].astype(F32)
    full = jnp.where(swapped, second, first).astype(BF16)
    part = jnp.where(swapped, first, second).astype(BF16)[:, 0:128]
    lane = lax.broadcasted_iota(jnp.int32, (64, 256), 1)
    third = jnp.where(lane < n_third, third, jnp.broadcast_to(third[:, 0:1], (64, 256))).astype(BF16)
    for half in range(2):
        hsel[half, :, 0:128] = full[:, 128 * half : 128 * half + 128]
        hsel[2 + half, :, 0:128] = third[:, 128 * half : 128 * half + 128]
        hsel[half, :, 128:256] = part
        hsel[2 + half, :, 128:256] = part

    pl.semaphore_wait(bar, 15 + 30)

    for i in range(1, NZ):
        send(dense.at[:, features], dense_rows(z, c), d_s.at[i - 1], d_r.at[enc],
             device((z + (1, 7, 2, 6, 3, 5, 4)[i - 1]) % NZ, c, x, y))
    send(dense.at[:, features], dense_rows(z, c), ds_s.at[z], d_r.at[enc], sibling)

    h_to = hrecv.at[aligned(64 * v, 64), :]

    def hidden_dest(i):
        j = (8 * (x % 2) + 2 * y + c + i) % 16
        return j // 8, (j // 2) % 4, j % 2

    for i in range(16):
        kind, yd, cd = hidden_dest(i)
        xd = 2 * c + kind
        src = hsel.at[2 * kind + cd]
        mine = jnp.logical_and(cd == c, jnp.logical_and(xd == x, yd == y))

        @pl.when(mine)
        def _():
            pltpu.make_async_copy(src, h_to, h_r.at[v]).start()

        @pl.when(jnp.logical_not(mine))
        def _():
            send(src, h_to, h_s.at[i], h_r.at[v], device(z, cd, xd, yd))

    for n, i in enumerate(AWAY):
        to = (enc + i) % NE
        send(weight.at[:, pl.ds(first_col(to), CW)], w_rows(x, enc), w_s.at[n], w_r.at[enc],
             device(to // 2, to % 2, x, y))
    for n, i in enumerate(AWAY):
        to = (enc + i) % NE
        send(queries.at[:, pl.ds(first_col(to), CW)], q_part(enc), q_s.at[n], q_r.at[enc],
             device(to // 2, to % 2, x, y))

    def weights_first(k):
        zz = zs[k]
        if k == 0:
            own_w.wait()
            arrived(w_rows(x, 2 * z + 1 - c), w_r.at[2 * z + 1 - c])
        else:
            arrived(w_rows(x, 2 * zz), w_r.at[2 * zz])
            arrived(w_rows(x, 2 * zz + 1), w_r.at[2 * zz + 1])
        pair, sem = w_pair(x, zz), wx_r.at[8 * x + zz]
        send(pair, pair, wx_s.at[3 * k], sem, device(z, c, xr, y))
        send(pair, pair, wx_s.at[3 * k + 1], sem, device(z, c, xl, y))

    def weights_second(k):
        zz = zs[k]
        arrived(w_pair(xl, zz), wx_r.at[8 * xl + zz])
        arrived(w_pair(xr, zz), wx_r.at[8 * xr + zz])
        origin, to = (xl, xr) if k % 2 == 0 else (xr, xl)
        pair = w_pair(origin, zz)
        send(pair, pair, wx_s.at[3 * k + 2], wx_r.at[8 * origin + zz], device(z, c, to, y))

    def rows_of(zz, yy):
        return tb.at[zz, aligned(ROWS * c, ROWS), aligned(FW * yy, FW)]

    def core_rows(zz, cc):
        return tb.at[zz, aligned(ROWS * cc, ROWS), :]

    def ring_sends(k, rows, sems, base, sem):
        if k == 0:
            send(rows, rows, sems.at[0], sem, up)
            send(rows, rows, sems.at[6], sem, down)
        elif k % 2 == 1 and k < 7:
            send(rows, rows, sems.at[k], sem, up)
        elif k % 2 == 0 and k < 6:
            send(rows, rows, sems.at[k], sem, down)

    def tokens_first(k):
        zz = zs[k]
        rows, sem = rows_of(zz, y), t_r.at[4 * zz + y]
        if k:
            arrived(rows, sem)
        ring_sends(k, rows, tz_s, 0, sem)
        send(rows, rows, ty_s.at[3 * k], sem, device(z, c, x, yr))
        send(rows, rows, ty_s.at[3 * k + 1], sem, device(z, c, x, yl))

    def tokens_second(k):
        zz = zs[k]
        arrived(rows_of(zz, yl), t_r.at[4 * zz + yl])
        arrived(rows_of(zz, yr), t_r.at[4 * zz + yr])
        origin, to = (yl, yr) if k % 2 == 0 else (yr, yl)
        rows = rows_of(zz, origin)
        send(rows, rows, ty_s.at[3 * k + 2], t_r.at[4 * zz + origin], device(z, c, x, to))

    def tokens_third(k):
        zz = zs[k]
        arrived(rows_of(zz, yo), t_r.at[4 * zz + yo])
        rows = core_rows(zz, c)
        send(rows, rows, ts_s.at[k], ts_r.at[zz], sibling)

    def queries_ring(k):
        zz = zs[k]
        rows, sem = q_rows(zz, c), g_r.at[2 * zz + c]
        if k:
            arrived(rows, sem)
        else:
            own_rows.wait()
        ring_sends(k, rows, g_s, 0, sem)
        send(rows, rows, gs_s.at[k], sem, sibling)

    def dense_gather():
        for k in range(1, NZ):
            rows, sem = dense_rows(zs[k], c), d_r.at[2 * zs[k] + c]
            arrived(rows, sem)
            send(rows, rows, ds_s.at[zs[k]], sem, sibling)
        own_dense.wait()
        for zz in range(NZ):
            arrived(dense_rows(zz, 1 - c), d_r.at[2 * zz + 1 - c])

    def dense_layer():
        for vv in range(NV):
            arrived(hrecv.at[pl.ds(64 * vv, 64), :], h_r.at[vv])
        xrows[...] = hrecv[...].astype(F32).T
        own = jnp.concatenate(
            [xrows[0:BIG, :], xrows[pl.ds(pl.multiple_of(BIG + SHORT * c, SHORT), SHORT), :]], axis=0
        ).astype(BF16)
        pre_act = jnp.dot(own, dn[...], preferred_element_type=F32)
        activated = 0.5 * pre_act * (1.0 + lax.erf(pre_act * np.float32(np.sqrt(0.5))))
        act[...] = activated
        center = jnp.mean(activated, axis=-1, keepdims=True)
        square = jnp.sum(jnp.square(activated - center), axis=-1, keepdims=True)
        lane = lax.broadcasted_iota(jnp.int32, (ROWS, 128), 1)
        stat[0:ROWS, :] = jnp.where(lane == 0, center, square)
        stat[ROWS:256, :] = jnp.zeros((256 - ROWS, 128), F32)
        stat_all[y] = stat[...].T[0:8, :]
        for i in range(1, NY):
            send(stat_all.at[y], stat_all.at[y], st_s.at[i - 1], st_r.at[y],
                 device(z, c, x, (y + i) % NY))

    def normalize():
        for i in range(1, NY):
            arrived(stat_all.at[(y + i) % NY], st_r.at[(y + i) % NY])
        centers, squares = stat_all[:, 0:1, :], stat_all[:, 1:2, :]
        center = jnp.mean(centers, axis=0)
        spread = jnp.sum(squares + FW * jnp.square(centers - center[None]), axis=0) * (1.0 / D)
        scale = lax.rsqrt(spread + 1e-05)
        row = lax.broadcasted_iota(jnp.int32, (128, 256), 0)
        both = jnp.where(
            row == 0, jnp.broadcast_to(center, (128, 256)), jnp.broadcast_to(scale, (128, 256))
        ).T
        normed = (act[...] - both[0:ROWS, 0:1]) * both[0:ROWS, 1:2]
        tb[z, aligned(ROWS * c, ROWS), features] = normed.astype(BF16)

    weights_first(0)
    dense_gather()
    weights_first(1)
    weights_first(2)
    dense_layer()
    weights_second(0)
    normalize()
    tokens_first(0)
    weights_first(3)
    weights_first(4)
    weights_second(1)
    tokens_first(1)
    tokens_first(2)
    tokens_second(0)
    weights_second(2)
    weights_first(5)
    weights_first(6)
    tokens_first(3)
    tokens_first(4)
    tokens_second(1)
    tokens_second(2)
    weights_first(7)
    weights_second(3)
    weights_second(4)
    tokens_first(5)
    tokens_first(6)
    tokens_first(7)
    for k in (3, 4, 5, 6, 7):
        tokens_second(k)
        tokens_third(k - 3)
        if k > 4:
            weights_second(k)
    queries_ring(0)
    for k in (5, 6, 7):
        tokens_third(k)
    for k in range(1, NZ):
        queries_ring(k)

    for zz in range(NZ):
        arrived(core_rows(zz, 1 - c), ts_r.at[zz])

    def over_columns(i, _):
        xx = (x + i + i // 2 - 2 * (i // 3)) % NX

        @pl.when(i == 3)
        def _():
            for zz in range(NZ):
                arrived(w_pair(xo, zz), wx_r.at[8 * xo + zz])

        def over_rows(h, _):
            logits = jnp.dot(
                tb[pl.ds(4 * h, 4)].reshape(8 * ROWS, D), wx[xx], preferred_element_type=F32
            ).reshape(8, ROWS, CW)
            for u in range(4):
                top = jnp.maximum(
                    jnp.max(logits[2 * u, 0:BIG], axis=0, keepdims=True),
                    jnp.max(logits[2 * u + 1, 0:BIG], axis=0, keepdims=True),
                )
                low = jnp.maximum(
                    jnp.max(logits[2 * u, BIG:ROWS], axis=0, keepdims=True),
                    jnp.max(logits[2 * u + 1, BIG:ROWS], axis=0, keepdims=True),
                )
                pool[xx, pl.ds(4 * h + u, 1), :] = top
                pool[xx, pl.ds(8 + 4 * h + u, 1), :] = low
            return 0

        lax.fori_loop(0, 2, over_rows, 0)
        return 0

    lax.fori_loop(0, NX, over_columns, 0)

    for i in range(1, NX):
        to = (x + i) % NX
        send(pool.at[to], mx.at[x], p_s.at[i - 1], p_r.at[x], device(z, c, to, y))
    mx[x] = pool[x]
    own_q.wait()
    own_bias.wait()
    for i in range(1, NE):
        fr = (enc + i) % NE
        arrived(q_part(fr), q_r.at[fr])
    for i in range(1, NX):
        fr = (x + i) % NX
        arrived(mx.at[fr], p_r.at[fr])
    peaks = jnp.concatenate(
        [mx[0, 0:8], mx[2, 0:8], mx[0, 8:16], mx[2, 8:16], mx[1, 0:8], mx[3, 0:8]], axis=0
    ) + biasv[...]
    reps = jnp.log1p(jnp.maximum(peaks, 0.0)).astype(BF16)
    rfull[enc] = reps

    def reps_ring(k):
        zz = zs[k]
        rows, sem = rfull.at[2 * zz + c], r_r.at[2 * zz + c]
        if k:
            arrived(rows, sem)
        ring_sends(k, rows, r_s, 0, sem)
        send(rows, rows, rs_s.at[k], sem, sibling)

    col = lax.broadcasted_iota(jnp.int32, (REPS, CW), 1)
    doubled = jnp.where(enc == NE - 1, NE * CW - COLS, 0)
    counted = jnp.where(col < doubled, 0.0, reps.astype(F32)).astype(BF16)
    sp[...] = lax.dot_general(
        counted, qall[...], (((1,), (1,)), ((), ())), preferred_element_type=F32
    )

    swapped = jnp.where(jnp.full((8, NQ), lens[0], jnp.int32) < 256, 1.0, 0.0)
    cbuf[0, 0:HALF, :] = sp[aligned(HALF * (1 - c), HALF), :]
    cbuf[0, HALF : HALF + 8, :] = swapped
    send(cbuf.at[0], cbuf.at[1], c_s.at[0], c_r.at[0], sibling)
    reps_ring(0)
    arrived(cbuf.at[1], c_r.at[0])
    xbuf[x] = sp[aligned(HALF * c, HALF), :] + cbuf[1, 0:HALF, :]
    theirs = cbuf[1, HALF : HALF + 8, :]
    for i in range(1, NX):
        send(xbuf.at[x], xbuf.at[x], x_s.at[i - 1], x_r.at[x], device(z, c, (x + i) % NX, y))
    reps_ring(1)
    reps_ring(2)
    for i in range(1, NX):
        arrived(xbuf.at[(x + i) % NX], x_r.at[(x + i) % NX])
    ybuf[y] = (xbuf[0] + xbuf[1]) + (xbuf[2] + xbuf[3])
    for i in range(1, NY):
        send(ybuf.at[y], ybuf.at[y], y_s.at[i - 1], y_r.at[y], device(z, c, x, (y + i) % NY))
    reps_ring(3)
    reps_ring(4)
    for i in range(1, NY):
        arrived(ybuf.at[(y + i) % NY], y_r.at[(y + i) % NY])
    row = lax.broadcasted_iota(jnp.int32, (8, NQ), 0)
    zbuf[z, 0:HALF, :] = (ybuf[0] + ybuf[1]) + (ybuf[2] + ybuf[3])
    zbuf[z, HALF : HALF + 8, :] = jnp.where((row // 4) == c, swapped, theirs)
    for i, away in enumerate((1, 7, 2, 6, 3, 5, 4)):
        send(zbuf.at[z], zbuf.at[z], z_s.at[i], z_r.at[z], device((z + away) % NZ, c, x, y))
    for k in (5, 6, 7):
        reps_ring(k)
    for i in range(1, NZ):
        arrived(zbuf.at[(z + i) % NZ], z_r.at[(z + i) % NZ])
    fin[aligned(HALF * c, HALF), :] = jnp.sum(zbuf[:, 0:HALF, :], axis=0)
    half = fin.at[aligned(HALF * c, HALF), :]
    send(half, half, c_s.at[1], c_r.at[1], sibling)
    flips = jnp.concatenate(
        [zbuf[zz, HALF + 4 * cc : HALF + 4 * cc + 1, :] for cc in range(2) for zz in range(NZ)],
        axis=0,
    )
    block = lax.broadcasted_iota(jnp.int32, (NE, NQ), 0)
    base = 3 * (2 * (block % 8) + block // 8)
    flip = jnp.where(flips > 0.5, 1, 0)
    passage = jnp.concatenate([base + flip, base + 1 - flip, base + 2], axis=0)
    is_positive = passage == positives[...]
    other = fin.at[aligned(HALF * (1 - c), HALF), :]
    arrived(other, c_r.at[1])

    scores = fin[...]
    peak = jnp.max(scores, axis=0, keepdims=True)
    log_total = jnp.log(jnp.sum(jnp.exp(scores - peak), axis=0, keepdims=True)) + peak
    picked = jnp.sum(jnp.where(is_positive, scores, 0.0), axis=0, keepdims=True)
    loss[...] = jnp.broadcast_to(
        jnp.sum(log_total - picked, axis=1, keepdims=True) * (1.0 / NQ), (8, NQ)
    )
    grad = jnp.exp(scores - log_total) - jnp.where(is_positive, 1.0, 0.0)
    sp[...] = grad
    gradT[...] = jnp.concatenate([grad, jnp.zeros((NQ - REPS, NQ), F32)], axis=0).T
    for_query = gradT[aligned(8 * enc, 8), 0:REPS].astype(BF16)
    block = 8 * c + z
    full_row, part_row = sp[pl.ds(block, 1), :], sp[pl.ds(16 + block, 1), :]
    last_row = sp[pl.ds(32 + block, 1), :]
    mine = swapped[0:1, :] > 0.5
    for_passage = jnp.concatenate(
        [
            jnp.where(mine, part_row, full_row),
            jnp.where(mine, full_row, part_row),
            last_row,
            jnp.zeros((5, NQ), F32),
        ],
        axis=0,
    ).astype(BF16)
    for zz in range(NZ):
        arrived(rfull.at[2 * zz + 1 - c], r_r.at[2 * zz + 1 - c])
        arrived(q_rows(zz, 1 - c), g_r.at[2 * zz + 1 - c])
    for ee in range(NE):
        skip = NE * CW - COLS if ee == NE - 1 else 0
        cols = slice(CW * ee, CW * (ee + 1) - skip)
        query_out[:, cols] = jnp.dot(for_query, rfull[ee], preferred_element_type=F32)[:, skip:]
        pass_out[:, cols] = jnp.dot(for_passage, qfull[:, cols], preferred_element_type=F32)[0:3]

    for i in range(NE - 1):
        arrived(w_rows(x, enc), w_s.at[i])
        arrived(q_part(enc), q_s.at[i])
    for i in range(16):
        kind, yd, cd = hidden_dest(i)
        mine = jnp.logical_and(cd == c, jnp.logical_and(2 * c + kind == x, yd == y))

        @pl.when(jnp.logical_not(mine))
        def _():
            arrived(hsel.at[0], h_s.at[i])

    for k in range(7):
        arrived(dense_rows(z, c), d_s.at[k])
        arrived(rows_of(z, y), tz_s.at[k])
        arrived(q_rows(z, c), g_s.at[k])
        arrived(rfull.at[enc], r_s.at[k])
        arrived(zbuf.at[z], z_s.at[k])
    for k in range(NZ):
        arrived(dense_rows(z, c), ds_s.at[k])
        arrived(core_rows(z, c), ts_s.at[k])
        arrived(q_rows(z, c), gs_s.at[k])
        arrived(rfull.at[enc], rs_s.at[k])
    for k in range(24):
        arrived(rows_of(z, y), ty_s.at[k])
        arrived(w_pair(x, z), wx_s.at[k])
    for k in range(3):
        arrived(stat_all.at[y], st_s.at[k])
        arrived(mx.at[x], p_s.at[k])
        arrived(xbuf.at[x], x_s.at[k])
        arrived(ybuf.at[y], y_s.at[k])
    arrived(cbuf.at[0], c_s.at[0])
    arrived(half, c_s.at[1])


def call(lens, hid, dense, weight, queries, bias, positives):
    def dma(*n):
        return [pltpu.SemaphoreType.DMA((k,)) for k in n]

    hbm = pl.BlockSpec(memory_space=pltpu.HBM)
    vm = pl.BlockSpec(memory_space=pltpu.VMEM)
    return pl.pallas_call(
        kernel,
        out_shape=(
            jax.ShapeDtypeStruct((8, NQ), F32),
            jax.ShapeDtypeStruct((8, COLS), F32),
            jax.ShapeDtypeStruct((3, COLS), F32),
        ),
        in_specs=[pl.BlockSpec(memory_space=pltpu.SMEM), hbm, hbm, hbm, hbm, hbm, vm],
        out_specs=(vm, vm, vm),
        scratch_shapes=[
            pltpu.VMEM((64, 768), BF16),
            pltpu.VMEM((4, 64, 256), BF16),
            pltpu.VMEM((D, 256), BF16),
            pltpu.VMEM((256, D), F32),
            pltpu.VMEM((D, FW), BF16),
            pltpu.VMEM((ROWS, FW), F32),
            pltpu.VMEM((256, 128), F32),
            pltpu.VMEM((NY, 8, 256), F32),
            pltpu.VMEM((NZ, 2 * ROWS, D), BF16),
            pltpu.VMEM((NX, D, CW), BF16),
            pltpu.VMEM((NX, 16, CW), F32),
            pltpu.VMEM((NX, 16, CW), F32),
            pltpu.VMEM((NQ, CW), BF16),
            pltpu.VMEM((NQ, COLS), BF16),
            pltpu.VMEM((NE, REPS, CW), BF16),
            pltpu.VMEM((1, CW), F32),
            pltpu.VMEM((REPS, NQ), F32),
            pltpu.VMEM((2, HALF + 8, NQ), F32),
            pltpu.VMEM((NX, HALF, NQ), F32),
            pltpu.VMEM((NY, HALF, NQ), F32),
            pltpu.VMEM((NZ, HALF + 8, NQ), F32),
            pltpu.VMEM((REPS, NQ), F32),
            pltpu.VMEM((NQ, NQ), F32),
        ]
        + dma(6, 16, 16, 7, 16, 8, 15, 16, 15, 16, 3, 4)
        + dma(7, 24, 32, 8, 8, 24, 32, 7, 16, 8, 3, 4)
        + dma(7, 16, 8, 2, 2, 3, 4, 3, 4, 7, 8),
        compiler_params=pltpu.CompilerParams(
            collective_id=0, has_side_effects=True, vmem_limit_bytes=48 << 20
        ),
        name="splade_head",
    )(lens, hid, dense, weight, queries, bias, positives)


def per_device(hidden, dense_weight, head_weight, head_bias, lengths, queries, positives):
    loss, query_grad, passage_grad = call(
        lengths, hidden.T, dense_weight, head_weight, queries,
        head_bias.reshape(1, COLS), positives.reshape(1, NQ),
    )
    return loss[0, 0], query_grad, passage_grad


def solution(mesh):
    placed = (
        P("enc", ("vocab", "grp")),
        P("enc", None),
        P("enc", ("vocab", "grp")),
        P(("vocab", "grp")),
        P("enc"),
        P("enc", ("vocab", "grp")),
        P(),
    )
    return jax.shard_map(
        per_device,
        mesh=mesh,
        in_specs=placed,
        out_specs=(P(), P("enc", ("vocab", "grp")), P("enc", ("vocab", "grp"))),
        check_vma=False,
    )
```

```python
import jax
import jax.numpy as jnp
import numpy as np
from jax import lax
from jax.experimental import pallas as pl
from jax.experimental.pallas import tpu as pltpu
from jax.sharding import PartitionSpec as P

NX, NY, NZ = 4, 4, 8
NE, NV = 16, 16
D = 1024
FW = D // NY
COLS = 7936
CW = 512
BIG, SHORT = 128, 16
ROWS = BIG + SHORT
NQ = 128
REPS = 48
HALF = REPS // 2
MESH = pl.DeviceIdType.MESH
F32, BF16 = jnp.float32, jnp.bfloat16


def place():
    enc, vocab, grp = lax.axis_index("enc"), lax.axis_index("vocab"), lax.axis_index("grp")
    return enc // 2, enc % 2, vocab // 2, (vocab % 2) * 2 + grp


def device(z, c, x, y):
    return (2 * z + c, 2 * x + y // 2, y % 2)


def first_col(enc):
    return pl.multiple_of(jnp.minimum(CW * enc, COLS - CW), 128)


def aligned(start, size):
    return pl.ds(pl.multiple_of(start, size), size)


def arrived(ref, sem):
    pltpu.make_async_copy(ref, ref, sem).wait()


def send(src, dst, send_sem, recv_sem, to):
    pltpu.make_async_remote_copy(
        src_ref=src, dst_ref=dst, send_sem=send_sem, recv_sem=recv_sem,
        device_id=to, device_id_type=MESH,
    ).start()


def ring_order(z):
    return [(z + off + NZ) % NZ for off in (0, -1, 1, -2, 2, -3, 3, -4)]


def kernel(
    lens, hid, dense, weight, queries, bias, positives, loss, query_out, pass_out,
    hidv, hsel, hrecv, xrows, dn, act, stat, stat_all, tb, wx, pool, mx, qall, qfull, rfull,
    biasv, sp, cbuf, xbuf, ybuf, zbuf, fin, gradT,
    loc, h_s, h_r, d_s, d_r, ds_s, w_s, w_r, q_s, q_r, st_s, st_r,
    tz_s, ty_s, t_r, ts_s, ts_r, wx_s, wx_r, g_s, g_r, gs_s, p_s, p_r,
    r_s, r_r, rs_s, c_s, c_r, x_s, x_r, y_s, y_r, z_s, z_r,
):
    z, c, x, y = place()
    enc, v = 2 * z + c, 4 * x + y
    zs = ring_order(z)
    up, down = device((z + 1) % NZ, c, x, y), device((z + NZ - 1) % NZ, c, x, y)
    sibling = device(z, 1 - c, x, y)
    xr, xl, xo = (x + 1) % NX, (x + 3) % NX, (x + 2) % NX
    yr, yl, yo = (y + 1) % NY, (y + 3) % NY, (y + 2) % NY
    features = aligned(FW * y, FW)

    def dense_rows(zz, cc):
        return dn.at[aligned(64 * (2 * zz + cc), 64), :]

    def q_part(ee):
        return qall.at[aligned(8 * ee, 8), :]

    def w_rows(xx, ee):
        return wx.at[xx, aligned(64 * ee, 64), :]

    def w_pair(xx, zz):
        return wx.at[xx, aligned(128 * zz, 128), :]

    def q_rows(zz, cc):
        return qfull.at[aligned(8 * (2 * zz + cc), 8), :]

    own_hid = pltpu.make_async_copy(hid, hidv, loc.at[0])
    own_hid.start()
    own_cols = pl.ds(first_col(enc), CW)
    own_dense = pltpu.make_async_copy(dense.at[:, features], dense_rows(z, c), loc.at[1])
    own_w = pltpu.make_async_copy(weight.at[:, own_cols], w_rows(x, enc), loc.at[2])
    own_q = pltpu.make_async_copy(queries.at[:, own_cols], q_part(enc), loc.at[3])
    own_rows = pltpu.make_async_copy(queries, q_rows(z, c), loc.at[4])
    own_bias = pltpu.make_async_copy(bias.at[:, own_cols], biasv, loc.at[5])
    for copy in (own_dense, own_w, own_q, own_rows, own_bias):
        copy.start()

    bar = pltpu.get_barrier_semaphore()
    for i in range(1, NE):
        to = (enc + i) % NE
        pl.semaphore_signal(
            bar, inc=1, device_id=device(to // 2, to % 2, x, y), device_id_type=MESH
        )
    for i in range(1, 2 * NV):
        if i != NV:
            at = (16 * c + v + i) % 32
            pl.semaphore_signal(
                bar, inc=1, device_id=device(z, at // 16, (at // 4) % 4, at % 4),
                device_id_type=MESH,
            )

    own_hid.wait()
    n_first, n_third = lens[0], lens[2]
    swapped = jnp.full((64, 256), n_first, jnp.int32) < 256
    first, second = hidv[:, 0:256].astype(F32), hidv[:, 256:512].astype(F32)
    third = hidv[:, 512:768].astype(F32)
    full = jnp.where(swapped, second, first).astype(BF16)
    part = jnp.where(swapped, first, second).astype(BF16)[:, 0:128]
    lane = lax.broadcasted_iota(jnp.int32, (64, 256), 1)
    third = jnp.where(lane < n_third, third, jnp.broadcast_to(third[:, 0:1], (64, 256))).astype(BF16)
    for half in range(2):
        hsel[half, :, 0:128] = full[:, 128 * half : 128 * half + 128]
        hsel[2 + half, :, 0:128] = third[:, 128 * half : 128 * half + 128]
        hsel[half, :, 128:256] = part
        hsel[2 + half, :, 128:256] = part

    pl.semaphore_wait(bar, 15 + 30)

    for i in range(1, NZ):
        send(dense.at[:, features], dense_rows(z, c), d_s.at[i - 1], d_r.at[enc],
             device((z + (1, 7, 2, 6, 3, 5, 4)[i - 1]) % NZ, c, x, y))
    send(dense.at[:, features], dense_rows(z, c), ds_s.at[z], d_r.at[enc], sibling)

    h_to = hrecv.at[aligned(64 * v, 64), :]

    def hidden_dest(i):
        j = (8 * (x % 2) + 2 * y + c + i) % 16
        return j // 8, (j // 2) % 4, j % 2

    for i in range(16):
        kind, yd, cd = hidden_dest(i)
        xd = 2 * c + kind
        src = hsel.at[2 * kind + cd]
        mine = jnp.logical_and(cd == c, jnp.logical_and(xd == x, yd == y))

        @pl.when(mine)
        def _():
            pltpu.make_async_copy(src, h_to, h_r.at[v]).start()

        @pl.when(jnp.logical_not(mine))
        def _():
            send(src, h_to, h_s.at[i], h_r.at[v], device(z, cd, xd, yd))

    def weights_out(far):
        for zz in ((z + far) % NZ, (z + NZ - far) % NZ)[: 1 if far in (0, 4) else 2]:
            for cc in (1 - c,) if far == 0 else (c, 1 - c):
                to = 2 * zz + cc
                send(weight.at[:, pl.ds(first_col(to), CW)], w_rows(x, enc), w_s.at[to],
                     w_r.at[enc], device(zz, cc, x, y))


    def queries_out():
        for i in range(1, NE):
            to = (enc + i) % NE
            send(queries.at[:, pl.ds(first_col(to), CW)], q_part(enc), q_s.at[i], q_r.at[enc],
                 device(to // 2, to % 2, x, y))

    def weights_first(k):
        zz = zs[k]
        if k == 0:
            own_w.wait()
            arrived(w_rows(x, 2 * z + 1 - c), w_r.at[2 * z + 1 - c])
        else:
            arrived(w_rows(x, 2 * zz), w_r.at[2 * zz])
            arrived(w_rows(x, 2 * zz + 1), w_r.at[2 * zz + 1])
        pair, sem = w_pair(x, zz), wx_r.at[8 * x + zz]
        send(pair, pair, wx_s.at[3 * k], sem, device(z, c, xr, y))
        send(pair, pair, wx_s.at[3 * k + 1], sem, device(z, c, xl, y))

    def weights_second(k):
        zz = zs[k]
        arrived(w_pair(xl, zz), wx_r.at[8 * xl + zz])
        arrived(w_pair(xr, zz), wx_r.at[8 * xr + zz])
        origin, to = (xl, xr) if k % 2 == 0 else (xr, xl)
        pair = w_pair(origin, zz)
        send(pair, pair, wx_s.at[3 * k + 2], wx_r.at[8 * origin + zz], device(z, c, to, y))

    def rows_of(k, yy):
        return tb.at[k, aligned(ROWS * c, ROWS), aligned(FW * yy, FW)]

    def core_rows(k, cc):
        return tb.at[k, aligned(ROWS * cc, ROWS), :]

    def ring_sends(k, rows, sems, base, sem):
        if k == 0:
            send(rows, rows, sems.at[0], sem, up)
            send(rows, rows, sems.at[6], sem, down)
        elif k % 2 == 1 and k < 7:
            send(rows, rows, sems.at[k], sem, up)
        elif k % 2 == 0 and k < 6:
            send(rows, rows, sems.at[k], sem, down)

    def tokens_first(k):
        rows, sem = rows_of(k, y), t_r.at[4 * k + y]
        if k:
            arrived(rows, sem)
        if k == 0:
            send(rows, rows_of(1, y), tz_s.at[0], t_r.at[4 + y], up)
            send(rows, rows_of(2, y), tz_s.at[6], t_r.at[8 + y], down)
        elif k < 6:
            send(rows, rows_of(k + 2, y), tz_s.at[k], t_r.at[4 * (k + 2) + y], up if k % 2 else down)
        send(rows, rows, ty_s.at[3 * k], sem, device(z, c, x, yr))
        send(rows, rows, ty_s.at[3 * k + 1], sem, device(z, c, x, yl))

    def tokens_second(k):
        arrived(rows_of(k, yl), t_r.at[4 * k + yl])
        arrived(rows_of(k, yr), t_r.at[4 * k + yr])
        origin, to = (yl, yr) if k % 2 == 0 else (yr, yl)
        rows = rows_of(k, origin)
        send(rows, rows, ty_s.at[3 * k + 2], t_r.at[4 * k + origin], device(z, c, x, to))

    def tokens_third(k):
        arrived(rows_of(k, yo), t_r.at[4 * k + yo])
        rows = core_rows(k, c)
        send(rows, rows, ts_s.at[k], ts_r.at[k], sibling)

    def queries_ring(k):
        zz = zs[k]
        rows, sem = q_rows(zz, c), g_r.at[2 * zz + c]
        if k:
            arrived(rows, sem)
        else:
            own_rows.wait()
        ring_sends(k, rows, g_s, 0, sem)
        send(rows, rows, gs_s.at[k], sem, sibling)

    def dense_gather():
        for k in range(1, NZ):
            rows, sem = dense_rows(zs[k], c), d_r.at[2 * zs[k] + c]
            arrived(rows, sem)
            send(rows, rows, ds_s.at[zs[k]], sem, sibling)

    def hidden_here():
        for vv in range(NV):
            arrived(hrecv.at[pl.ds(64 * vv, 64), :], h_r.at[vv])
        xrows[...] = hrecv[...].astype(F32).T

    def dense_layer():
        own = jnp.concatenate(
            [xrows[0:BIG, :], xrows[aligned(BIG + SHORT * (2 * (x % 2) + c), SHORT), :]], axis=0
        ).astype(BF16)
        own_dense.wait()
        for zz in range(NZ):
            arrived(dense_rows(zz, 1 - c), d_r.at[2 * zz + 1 - c])
        pre_act = jnp.dot(own, dn[...], preferred_element_type=F32)
        activated = 0.5 * pre_act * (1.0 + lax.erf(pre_act * np.float32(np.sqrt(0.5))))
        act[...] = activated
        center = jnp.mean(activated, axis=-1, keepdims=True)
        square = jnp.sum(jnp.square(activated - center), axis=-1, keepdims=True)
        lane = lax.broadcasted_iota(jnp.int32, (ROWS, 128), 1)
        stat[0:ROWS, :] = jnp.where(lane == 0, center, square)
        stat[ROWS:256, :] = jnp.zeros((256 - ROWS, 128), F32)
        stat_all[y] = stat[...].T[0:8, :]
        for i in range(1, NY):
            send(stat_all.at[y], stat_all.at[y], st_s.at[i - 1], st_r.at[y],
                 device(z, c, x, (y + i) % NY))

    def normalize():
        for i in range(1, NY):
            arrived(stat_all.at[(y + i) % NY], st_r.at[(y + i) % NY])
        centers, squares = stat_all[:, 0:1, :], stat_all[:, 1:2, :]
        center = jnp.mean(centers, axis=0)
        spread = jnp.sum(squares + FW * jnp.square(centers - center[None]), axis=0) * (1.0 / D)
        scale = lax.rsqrt(spread + 1e-05)
        row = lax.broadcasted_iota(jnp.int32, (128, 256), 0)
        both = jnp.where(
            row == 0, jnp.broadcast_to(center, (128, 256)), jnp.broadcast_to(scale, (128, 256))
        ).T
        normed = (act[...] - both[0:ROWS, 0:1]) * both[0:ROWS, 1:2]
        tb[0, aligned(ROWS * c, ROWS), features] = normed.astype(BF16)

    def weights_here():
        for zz in range(NZ):
            arrived(w_pair(xo, zz), wx_r.at[8 * xo + zz])

    def pool_rows(first, size, xx):
        logits = jnp.dot(
            tb[first : first + size].reshape(size * 2 * ROWS, D), wx[xx],
            preferred_element_type=F32,
        ).reshape(2 * size, ROWS, CW)
        for u in range(size):
            zz = zs[first + u]
            pool[xx, pl.ds(zz, 1), :] = jnp.maximum(
                jnp.max(logits[2 * u, 0:BIG], axis=0, keepdims=True),
                jnp.max(logits[2 * u + 1, 0:BIG], axis=0, keepdims=True),
            )
            pool[xx, pl.ds(8 + zz, 1), :] = jnp.maximum(
                jnp.max(logits[2 * u, BIG:ROWS], axis=0, keepdims=True),
                jnp.max(logits[2 * u + 1, BIG:ROWS], axis=0, keepdims=True),
            )

    def pooled(n, size):
        for k in range(size * n, size * n + size):
            arrived(core_rows(k, 1 - c), ts_r.at[k])

        def over_columns(i, _):
            xx = (x + i + i // 2) % NX
            pool_rows(size * n, size, xx)
            if size * (n + 1) == NZ:

                @pl.when(i > 0)
                def _():
                    send(pool.at[xx], mx.at[x], p_s.at[i - 1], p_r.at[x], device(z, c, xx, y))

            return 0

        lax.fori_loop(0, NX - 1, over_columns, 0)

    def pooled_last():
        for first in (0, 4):
            pool_rows(first, 4, xo)
        send(pool.at[xo], mx.at[x], p_s.at[2], p_r.at[x], device(z, c, xo, y))

    weights_out(0)
    weights_out(1)
    weights_out(2)
    weights_first(0)
    dense_gather()
    weights_first(1)
    weights_first(2)
    weights_out(3)
    hidden_here()
    dense_layer()
    weights_first(3)
    weights_first(4)
    weights_out(4)
    normalize()
    tokens_first(0)
    weights_first(5)
    weights_first(6)
    tokens_first(1)
    tokens_first(2)
    tokens_second(0)
    weights_second(0)
    weights_second(1)
    weights_first(7)
    tokens_first(3)
    tokens_first(4)
    tokens_second(1)
    tokens_second(2)
    weights_second(2)
    weights_second(3)
    tokens_first(5)
    tokens_first(6)
    tokens_third(0)
    tokens_second(3)
    tokens_third(1)
    weights_second(4)
    tokens_second(4)
    tokens_third(2)
    tokens_first(7)
    weights_second(5)
    tokens_second(5)
    tokens_third(3)
    weights_second(6)
    tokens_second(6)
    tokens_third(4)
    weights_second(7)
    queries_out()
    queries_ring(0)
    pooled(0, 2)
    tokens_second(7)
    tokens_third(5)
    pooled(1, 2)
    tokens_third(6)
    tokens_third(7)
    queries_ring(1)
    queries_ring(2)
    pooled(2, 2)
    pooled(3, 2)
    queries_ring(3)
    queries_ring(4)
    weights_here()
    pooled_last()

    mx[x] = pool[x]
    own_bias.wait()
    for i in range(1, NX):
        fr = (x + i) % NX
        arrived(mx.at[fr], p_r.at[fr])
    peaks = jnp.concatenate(
        [
            mx[0, 0:8],
            mx[2, 0:8],
            jnp.maximum(mx[0, 8:16], mx[1, 8:16]),
            jnp.maximum(mx[2, 8:16], mx[3, 8:16]),
            mx[1, 0:8],
            mx[3, 0:8],
        ],
        axis=0,
    ) + biasv[...]
    reps = jnp.log1p(jnp.maximum(peaks, 0.0)).astype(BF16)
    rfull[enc] = reps

    def reps_ring(k):
        zz = zs[k]
        rows, sem = rfull.at[2 * zz + c], r_r.at[2 * zz + c]
        if k:
            arrived(rows, sem)
        ring_sends(k, rows, r_s, 0, sem)
        send(rows, rows, rs_s.at[k], sem, sibling)

    col = lax.broadcasted_iota(jnp.int32, (REPS, CW), 1)
    doubled = jnp.where(enc == NE - 1, NE * CW - COLS, 0)
    counted = jnp.where(col < doubled, 0.0, reps.astype(F32)).astype(BF16)
    own_q.wait()
    for i in range(1, NE):
        arrived(q_part((enc + i) % NE), q_r.at[(enc + i) % NE])
    sp[...] = lax.dot_general(
        counted, qall[...], (((1,), (1,)), ((), ())), preferred_element_type=F32
    )

    swapped = jnp.where(jnp.full((8, NQ), lens[0], jnp.int32) < 256, 1.0, 0.0)
    cbuf[0, 0:HALF, :] = sp[aligned(HALF * (1 - c), HALF), :]
    cbuf[0, HALF : HALF + 8, :] = swapped
    send(cbuf.at[0], cbuf.at[1], c_s.at[0], c_r.at[0], sibling)
    reps_ring(0)
    queries_ring(5)
    queries_ring(6)
    arrived(cbuf.at[1], c_r.at[0])
    xbuf[x] = sp[aligned(HALF * c, HALF), :] + cbuf[1, 0:HALF, :]
    theirs = cbuf[1, HALF : HALF + 8, :]
    for i in range(1, NX):
        send(xbuf.at[x], xbuf.at[x], x_s.at[i - 1], x_r.at[x], device(z, c, (x + i) % NX, y))
    reps_ring(1)
    reps_ring(2)
    queries_ring(7)
    for i in range(1, NX):
        arrived(xbuf.at[(x + i) % NX], x_r.at[(x + i) % NX])
    ybuf[y] = (xbuf[0] + xbuf[1]) + (xbuf[2] + xbuf[3])
    for i in range(1, NY):
        send(ybuf.at[y], ybuf.at[y], y_s.at[i - 1], y_r.at[y], device(z, c, x, (y + i) % NY))
    reps_ring(3)
    reps_ring(4)
    for i in range(1, NY):
        arrived(ybuf.at[(y + i) % NY], y_r.at[(y + i) % NY])
    row = lax.broadcasted_iota(jnp.int32, (8, NQ), 0)
    zbuf[z, 0:HALF, :] = (ybuf[0] + ybuf[1]) + (ybuf[2] + ybuf[3])
    zbuf[z, HALF : HALF + 8, :] = jnp.where((row // 4) == c, swapped, theirs)
    for i, away in enumerate((1, 7, 2, 6, 3, 5, 4)):
        send(zbuf.at[z], zbuf.at[z], z_s.at[i], z_r.at[z], device((z + away) % NZ, c, x, y))
    for k in (5, 6, 7):
        reps_ring(k)
    for i in range(1, NZ):
        arrived(zbuf.at[(z + i) % NZ], z_r.at[(z + i) % NZ])
    fin[aligned(HALF * c, HALF), :] = jnp.sum(zbuf[:, 0:HALF, :], axis=0)
    half = fin.at[aligned(HALF * c, HALF), :]
    send(half, half, c_s.at[1], c_r.at[1], sibling)
    flips = jnp.concatenate(
        [zbuf[zz, HALF + 4 * cc : HALF + 4 * cc + 1, :] for cc in range(2) for zz in range(NZ)],
        axis=0,
    )
    block = lax.broadcasted_iota(jnp.int32, (NE, NQ), 0)
    base = 3 * (2 * (block % 8) + block // 8)
    flip = jnp.where(flips > 0.5, 1, 0)
    passage = jnp.concatenate([base + flip, base + 1 - flip, base + 2], axis=0)
    is_positive = passage == positives[...]
    other = fin.at[aligned(HALF * (1 - c), HALF), :]
    arrived(other, c_r.at[1])

    scores = fin[...]
    peak = jnp.max(scores, axis=0, keepdims=True)
    log_total = jnp.log(jnp.sum(jnp.exp(scores - peak), axis=0, keepdims=True)) + peak
    picked = jnp.sum(jnp.where(is_positive, scores, 0.0), axis=0, keepdims=True)
    loss[...] = jnp.broadcast_to(
        jnp.sum(log_total - picked, axis=1, keepdims=True) * (1.0 / NQ), (8, NQ)
    )
    grad = jnp.exp(scores - log_total) - jnp.where(is_positive, 1.0, 0.0)
    sp[...] = grad
    gradT[...] = jnp.concatenate([grad, jnp.zeros((NQ - REPS, NQ), F32)], axis=0).T
    for_query = gradT[aligned(8 * enc, 8), 0:REPS].astype(BF16)
    block = 8 * c + z
    full_row, part_row = sp[pl.ds(block, 1), :], sp[pl.ds(16 + block, 1), :]
    last_row = sp[pl.ds(32 + block, 1), :]
    mine = swapped[0:1, :] > 0.5
    for_passage = jnp.concatenate(
        [
            jnp.where(mine, part_row, full_row),
            jnp.where(mine, full_row, part_row),
            last_row,
            jnp.zeros((5, NQ), F32),
        ],
        axis=0,
    ).astype(BF16)
    for zz in range(NZ):
        arrived(rfull.at[2 * zz + 1 - c], r_r.at[2 * zz + 1 - c])
        arrived(q_rows(zz, 1 - c), g_r.at[2 * zz + 1 - c])
    for ee in range(NE):
        skip = NE * CW - COLS if ee == NE - 1 else 0
        cols = slice(CW * ee, CW * (ee + 1) - skip)
        query_out[:, cols] = jnp.dot(for_query, rfull[ee], preferred_element_type=F32)[:, skip:]
        pass_out[:, cols] = jnp.dot(for_passage, qfull[:, cols], preferred_element_type=F32)[0:3]

    for i in range(1, NE):
        arrived(w_rows(x, enc), w_s.at[(enc + i) % NE])
        arrived(q_part(enc), q_s.at[i])
    for i in range(16):
        kind, yd, cd = hidden_dest(i)
        mine = jnp.logical_and(cd == c, jnp.logical_and(2 * c + kind == x, yd == y))

        @pl.when(jnp.logical_not(mine))
        def _():
            arrived(hsel.at[0], h_s.at[i])

    for k in range(7):
        arrived(dense_rows(z, c), d_s.at[k])
        arrived(rows_of(0, y), tz_s.at[k])
        arrived(q_rows(z, c), g_s.at[k])
        arrived(rfull.at[enc], r_s.at[k])
        arrived(zbuf.at[z], z_s.at[k])
    for k in range(NZ):
        arrived(dense_rows(z, c), ds_s.at[k])
        arrived(core_rows(0, c), ts_s.at[k])
        arrived(q_rows(z, c), gs_s.at[k])
        arrived(rfull.at[enc], rs_s.at[k])
    for k in range(24):
        arrived(rows_of(0, y), ty_s.at[k])
        arrived(w_pair(x, z), wx_s.at[k])
    for k in range(3):
        arrived(stat_all.at[y], st_s.at[k])
        arrived(mx.at[x], p_s.at[k])
        arrived(xbuf.at[x], x_s.at[k])
        arrived(ybuf.at[y], y_s.at[k])
    arrived(cbuf.at[0], c_s.at[0])
    arrived(half, c_s.at[1])


def call(lens, hid, dense, weight, queries, bias, positives):
    def dma(*n):
        return [pltpu.SemaphoreType.DMA((k,)) for k in n]

    hbm = pl.BlockSpec(memory_space=pltpu.HBM)
    vm = pl.BlockSpec(memory_space=pltpu.VMEM)
    return pl.pallas_call(
        kernel,
        out_shape=(
            jax.ShapeDtypeStruct((8, NQ), F32),
            jax.ShapeDtypeStruct((8, COLS), F32),
            jax.ShapeDtypeStruct((3, COLS), F32),
        ),
        in_specs=[pl.BlockSpec(memory_space=pltpu.SMEM), hbm, hbm, hbm, hbm, hbm, vm],
        out_specs=(vm, vm, vm),
        scratch_shapes=[
            pltpu.VMEM((64, 768), BF16),
            pltpu.VMEM((4, 64, 256), BF16),
            pltpu.VMEM((D, 256), BF16),
            pltpu.VMEM((256, D), F32),
            pltpu.VMEM((D, FW), BF16),
            pltpu.VMEM((ROWS, FW), F32),
            pltpu.VMEM((256, 128), F32),
            pltpu.VMEM((NY, 8, 256), F32),
            pltpu.VMEM((NZ, 2 * ROWS, D), BF16),
            pltpu.VMEM((NX, D, CW), BF16),
            pltpu.VMEM((NX, 16, CW), F32),
            pltpu.VMEM((NX, 16, CW), F32),
            pltpu.VMEM((NQ, CW), BF16),
            pltpu.VMEM((NQ, COLS), BF16),
            pltpu.VMEM((NE, REPS, CW), BF16),
            pltpu.VMEM((1, CW), F32),
            pltpu.VMEM((REPS, NQ), F32),
            pltpu.VMEM((2, HALF + 8, NQ), F32),
            pltpu.VMEM((NX, HALF, NQ), F32),
            pltpu.VMEM((NY, HALF, NQ), F32),
            pltpu.VMEM((NZ, HALF + 8, NQ), F32),
            pltpu.VMEM((REPS, NQ), F32),
            pltpu.VMEM((NQ, NQ), F32),
        ]
        + dma(6, 16, 16, 7, 16, 8, 16, 16, 16, 16, 3, 4)
        + dma(7, 24, 32, 8, 8, 24, 32, 7, 16, 8, 3, 4)
        + dma(7, 16, 8, 2, 2, 3, 4, 3, 4, 7, 8),
        compiler_params=pltpu.CompilerParams(
            collective_id=0, has_side_effects=True, vmem_limit_bytes=48 << 20
        ),
        name="splade_head",
    )(lens, hid, dense, weight, queries, bias, positives)


def per_device(hidden, dense_weight, head_weight, head_bias, lengths, queries, positives):
    loss, query_grad, passage_grad = call(
        lengths, hidden.T, dense_weight, head_weight, queries,
        head_bias.reshape(1, COLS), positives.reshape(1, NQ),
    )
    return loss[0, 0], query_grad, passage_grad


def solution(mesh):
    placed = (
        P("enc", ("vocab", "grp")),
        P("enc", None),
        P("enc", ("vocab", "grp")),
        P(("vocab", "grp")),
        P("enc"),
        P("enc", ("vocab", "grp")),
        P(),
    )
    return jax.shard_map(
        per_device,
        mesh=mesh,
        in_specs=placed,
        out_specs=(P(), P("enc", ("vocab", "grp")), P("enc", ("vocab", "grp"))),
        check_vma=False,
    )
```

```python
import jax
import jax.numpy as jnp
import numpy as np
from jax import lax
from jax.experimental import pallas as pl
from jax.experimental.pallas import tpu as pltpu
from jax.sharding import PartitionSpec as P

NX, NY, NZ = 4, 4, 8
NE, NV = 16, 16
D = 1024
FW = D // NY
COLS = 7936
CW = 512
BIG, SHORT = 128, 16
ROWS = BIG + SHORT
NQ = 128
REPS = 48
HALF = REPS // 2
MESH = pl.DeviceIdType.MESH
F32, BF16 = jnp.float32, jnp.bfloat16


def place():
    enc, vocab, grp = lax.axis_index("enc"), lax.axis_index("vocab"), lax.axis_index("grp")
    return enc // 2, enc % 2, vocab // 2, (vocab % 2) * 2 + grp


def device(z, c, x, y):
    return (2 * z + c, 2 * x + y // 2, y % 2)


def first_col(enc):
    return pl.multiple_of(jnp.minimum(CW * enc, COLS - CW), 128)


def aligned(start, size):
    return pl.ds(pl.multiple_of(start, size), size)


def arrived(ref, sem):
    pltpu.make_async_copy(ref, ref, sem).wait()


def send(src, dst, send_sem, recv_sem, to):
    pltpu.make_async_remote_copy(
        src_ref=src, dst_ref=dst, send_sem=send_sem, recv_sem=recv_sem,
        device_id=to, device_id_type=MESH,
    ).start()


def ring_order(z):
    return [(z + off + NZ) % NZ for off in (0, -1, 1, -2, 2, -3, 3, -4)]


def kernel(
    lens, hid, dense, weight, queries, bias, positives, loss, query_out, pass_out,
    hidv, hsel, hrecv, xrows, dn, act, stat, stat_all, tb, wx, pool, mx, qall, qfull, rfull,
    biasv, sp, cbuf, xbuf, ybuf, zbuf, fin, gradT,
    loc, h_s, h_r, d_s, d_r, ds_s, w_s, w_r, q_s, q_r, st_s, st_r,
    tz_s, ty_s, t_r, ts_s, ts_r, wx_s, wx_r, g_s, g_r, gs_s, p_s, p_r,
    r_s, r_r, rs_s, c_s, c_r, x_s, x_r, y_s, y_r, z_s, z_r,
):
    z, c, x, y = place()
    enc, v = 2 * z + c, 4 * x + y
    zs = ring_order(z)
    up, down = device((z + 1) % NZ, c, x, y), device((z + NZ - 1) % NZ, c, x, y)
    sibling = device(z, 1 - c, x, y)
    xr, xl, xo = (x + 1) % NX, (x + 3) % NX, (x + 2) % NX
    yr, yl, yo = (y + 1) % NY, (y + 3) % NY, (y + 2) % NY
    features = aligned(FW * y, FW)

    def dense_rows(zz, cc):
        return dn.at[aligned(64 * (2 * zz + cc), 64), :]

    def q_part(ee):
        return qall.at[aligned(8 * ee, 8), :]

    def w_rows(xx, ee):
        return wx.at[xx, aligned(64 * ee, 64), :]

    def w_pair(xx, zz):
        return wx.at[xx, aligned(128 * zz, 128), :]

    def q_rows(zz, cc):
        return qfull.at[aligned(8 * (2 * zz + cc), 8), :]

    own_hid = pltpu.make_async_copy(hid, hidv, loc.at[0])
    own_hid.start()
    own_cols = pl.ds(first_col(enc), CW)
    own_dense = pltpu.make_async_copy(dense.at[:, features], dense_rows(z, c), loc.at[1])
    own_w = pltpu.make_async_copy(weight.at[:, own_cols], w_rows(x, enc), loc.at[2])
    own_q = pltpu.make_async_copy(queries.at[:, own_cols], q_part(enc), loc.at[3])
    own_rows = pltpu.make_async_copy(queries, q_rows(z, c), loc.at[4])
    own_bias = pltpu.make_async_copy(bias.at[:, own_cols], biasv, loc.at[5])
    for copy in (own_dense, own_w, own_q, own_rows, own_bias):
        copy.start()

    bar = pltpu.get_barrier_semaphore()
    for i in range(1, NE):
        to = (enc + i) % NE
        pl.semaphore_signal(
            bar, inc=1, device_id=device(to // 2, to % 2, x, y), device_id_type=MESH
        )
    for i in range(1, 2 * NV):
        if i != NV:
            at = (16 * c + v + i) % 32
            pl.semaphore_signal(
                bar, inc=1, device_id=device(z, at // 16, (at // 4) % 4, at % 4),
                device_id_type=MESH,
            )

    own_hid.wait()
    n_first, n_third = lens[0], lens[2]
    swapped = jnp.full((64, 256), n_first, jnp.int32) < 256
    first, second = hidv[:, 0:256].astype(F32), hidv[:, 256:512].astype(F32)
    third = hidv[:, 512:768].astype(F32)
    full = jnp.where(swapped, second, first).astype(BF16)
    part = jnp.where(swapped, first, second).astype(BF16)[:, 0:128]
    lane = lax.broadcasted_iota(jnp.int32, (64, 256), 1)
    third = jnp.where(lane < n_third, third, jnp.broadcast_to(third[:, 0:1], (64, 256))).astype(BF16)
    for half in range(2):
        hsel[half, :, 0:128] = full[:, 128 * half : 128 * half + 128]
        hsel[2 + half, :, 0:128] = third[:, 128 * half : 128 * half + 128]
        hsel[half, :, 128:256] = part
        hsel[2 + half, :, 128:256] = part

    pl.semaphore_wait(bar, 15 + 30)

    for i in range(1, NZ):
        send(dense.at[:, features], dense_rows(z, c), d_s.at[i - 1], d_r.at[enc],
             device((z + (1, 7, 2, 6, 3, 5, 4)[i - 1]) % NZ, c, x, y))
    send(dense.at[:, features], dense_rows(z, c), ds_s.at[z], d_r.at[enc], sibling)

    h_to = hrecv.at[aligned(64 * v, 64), :]

    def hidden_dest(i):
        j = (8 * (x % 2) + 2 * y + c + i) % 16
        return j // 8, (j // 2) % 4, j % 2

    for i in range(16):
        kind, yd, cd = hidden_dest(i)
        xd = 2 * c + kind
        src = hsel.at[2 * kind + cd]
        mine = jnp.logical_and(cd == c, jnp.logical_and(xd == x, yd == y))

        @pl.when(mine)
        def _():
            pltpu.make_async_copy(src, h_to, h_r.at[v]).start()

        @pl.when(jnp.logical_not(mine))
        def _():
            send(src, h_to, h_s.at[i], h_r.at[v], device(z, cd, xd, yd))

    def weights_out(far):
        for zz in ((z + far) % NZ, (z + NZ - far) % NZ)[: 1 if far in (0, 4) else 2]:
            for cc in (1 - c,) if far == 0 else (c, 1 - c):
                to = 2 * zz + cc
                send(weight.at[:, pl.ds(first_col(to), CW)], w_rows(x, enc), w_s.at[to],
                     w_r.at[enc], device(zz, cc, x, y))


    def queries_out():
        for i in range(1, NE):
            to = (enc + i) % NE
            send(queries.at[:, pl.ds(first_col(to), CW)], q_part(enc), q_s.at[i], q_r.at[enc],
                 device(to // 2, to % 2, x, y))

    def weights_first(k):
        zz = zs[k]
        if k == 0:
            own_w.wait()
            arrived(w_rows(x, 2 * z + 1 - c), w_r.at[2 * z + 1 - c])
        else:
            arrived(w_rows(x, 2 * zz), w_r.at[2 * zz])
            arrived(w_rows(x, 2 * zz + 1), w_r.at[2 * zz + 1])
        pair, sem = w_pair(x, zz), wx_r.at[8 * x + zz]
        send(pair, pair, wx_s.at[3 * k], sem, device(z, c, xr, y))
        send(pair, pair, wx_s.at[3 * k + 1], sem, device(z, c, xl, y))

    def weights_second(k):
        zz = zs[k]
        arrived(w_pair(xl, zz), wx_r.at[8 * xl + zz])
        arrived(w_pair(xr, zz), wx_r.at[8 * xr + zz])
        origin, to = (xl, xr) if k % 2 == 0 else (xr, xl)
        pair = w_pair(origin, zz)
        send(pair, pair, wx_s.at[3 * k + 2], wx_r.at[8 * origin + zz], device(z, c, to, y))

    def rows_of(k, yy):
        return tb.at[k, aligned(ROWS * c, ROWS), aligned(FW * yy, FW)]

    def core_rows(k, cc):
        return tb.at[k, aligned(ROWS * cc, ROWS), :]

    def ring_sends(k, rows, sems, base, sem):
        if k == 0:
            send(rows, rows, sems.at[0], sem, up)
            send(rows, rows, sems.at[6], sem, down)
        elif k % 2 == 1 and k < 7:
            send(rows, rows, sems.at[k], sem, up)
        elif k % 2 == 0 and k < 6:
            send(rows, rows, sems.at[k], sem, down)

    def tokens_first(k):
        rows, sem = rows_of(k, y), t_r.at[4 * k + y]
        if k:
            arrived(rows, sem)
        if k == 0:
            send(rows, rows_of(1, y), tz_s.at[0], t_r.at[4 + y], up)
            send(rows, rows_of(2, y), tz_s.at[6], t_r.at[8 + y], down)
        elif k < 6:
            send(rows, rows_of(k + 2, y), tz_s.at[k], t_r.at[4 * (k + 2) + y], up if k % 2 else down)
        send(rows, rows, ty_s.at[3 * k], sem, device(z, c, x, yr))
        send(rows, rows, ty_s.at[3 * k + 1], sem, device(z, c, x, yl))

    def tokens_second(k):
        arrived(rows_of(k, yl), t_r.at[4 * k + yl])
        arrived(rows_of(k, yr), t_r.at[4 * k + yr])
        origin, to = (yl, yr) if k % 2 == 0 else (yr, yl)
        rows = rows_of(k, origin)
        send(rows, rows, ty_s.at[3 * k + 2], t_r.at[4 * k + origin], device(z, c, x, to))

    def tokens_third(k):
        arrived(rows_of(k, yo), t_r.at[4 * k + yo])
        rows = core_rows(k, c)
        send(rows, rows, ts_s.at[k], ts_r.at[k], sibling)

    def queries_ring(k):
        zz = zs[k]
        rows, sem = q_rows(zz, c), g_r.at[2 * zz + c]
        if k:
            arrived(rows, sem)
        else:
            own_rows.wait()
        ring_sends(k, rows, g_s, 0, sem)
        send(rows, rows, gs_s.at[k], sem, sibling)

    def dense_gather():
        for k in range(1, NZ):
            rows, sem = dense_rows(zs[k], c), d_r.at[2 * zs[k] + c]
            arrived(rows, sem)
            send(rows, rows, ds_s.at[zs[k]], sem, sibling)

    def hidden_here():
        for vv in range(NV):
            arrived(hrecv.at[pl.ds(64 * vv, 64), :], h_r.at[vv])
        xrows[...] = hrecv[...].astype(F32).T

    def dense_layer():
        own = jnp.concatenate(
            [xrows[0:BIG, :], xrows[aligned(BIG + SHORT * (2 * (x % 2) + c), SHORT), :]], axis=0
        ).astype(BF16)
        own_dense.wait()
        for zz in range(NZ):
            arrived(dense_rows(zz, 1 - c), d_r.at[2 * zz + 1 - c])
        pre_act = jnp.dot(own, dn[...], preferred_element_type=F32)
        activated = 0.5 * pre_act * (1.0 + lax.erf(pre_act * np.float32(np.sqrt(0.5))))
        act[...] = activated
        center = jnp.mean(activated, axis=-1, keepdims=True)
        square = jnp.sum(jnp.square(activated - center), axis=-1, keepdims=True)
        lane = lax.broadcasted_iota(jnp.int32, (ROWS, 128), 1)
        stat[0:ROWS, :] = jnp.where(lane == 0, center, square)
        stat[ROWS:256, :] = jnp.zeros((256 - ROWS, 128), F32)
        stat_all[y] = stat[...].T[0:8, :]
        for i in range(1, NY):
            send(stat_all.at[y], stat_all.at[y], st_s.at[i - 1], st_r.at[y],
                 device(z, c, x, (y + i) % NY))

    def normalize():
        for i in range(1, NY):
            arrived(stat_all.at[(y + i) % NY], st_r.at[(y + i) % NY])
        centers, squares = stat_all[:, 0:1, :], stat_all[:, 1:2, :]
        center = jnp.mean(centers, axis=0)
        spread = jnp.sum(squares + FW * jnp.square(centers - center[None]), axis=0) * (1.0 / D)
        scale = lax.rsqrt(spread + 1e-05)
        row = lax.broadcasted_iota(jnp.int32, (128, 256), 0)
        both = jnp.where(
            row == 0, jnp.broadcast_to(center, (128, 256)), jnp.broadcast_to(scale, (128, 256))
        ).T
        normed = (act[...] - both[0:ROWS, 0:1]) * both[0:ROWS, 1:2]
        tb[0, aligned(ROWS * c, ROWS), features] = normed.astype(BF16)

    def weights_here():
        for zz in range(NZ):
            arrived(w_pair(xo, zz), wx_r.at[8 * xo + zz])

    def pool_rows(first, size, xx):
        logits = jnp.dot(
            tb[first : first + size].reshape(size * 2 * ROWS, D), wx[xx],
            preferred_element_type=F32,
        ).reshape(2 * size, ROWS, CW)
        for u in range(size):
            zz = zs[first + u]
            pool[xx, pl.ds(zz, 1), :] = jnp.maximum(
                jnp.max(logits[2 * u, 0:BIG], axis=0, keepdims=True),
                jnp.max(logits[2 * u + 1, 0:BIG], axis=0, keepdims=True),
            )
            pool[xx, pl.ds(8 + zz, 1), :] = jnp.maximum(
                jnp.max(logits[2 * u, BIG:ROWS], axis=0, keepdims=True),
                jnp.max(logits[2 * u + 1, BIG:ROWS], axis=0, keepdims=True),
            )

    def pooled(n, size):
        for k in range(size * n, size * n + size):
            arrived(core_rows(k, 1 - c), ts_r.at[k])

        def over_columns(i, _):
            xx = (x + i + i // 2) % NX
            pool_rows(size * n, size, xx)
            if size * (n + 1) == NZ:

                @pl.when(i > 0)
                def _():
                    send(pool.at[xx], mx.at[x], p_s.at[i - 1], p_r.at[x], device(z, c, xx, y))

            return 0

        lax.fori_loop(0, NX - 1, over_columns, 0)

    def pooled_last():
        for first in (0, 4):
            pool_rows(first, 4, xo)
        send(pool.at[xo], mx.at[x], p_s.at[2], p_r.at[x], device(z, c, xo, y))

    weights_out(0)
    weights_out(1)
    weights_out(2)
    weights_first(0)
    dense_gather()
    weights_first(1)
    weights_first(2)
    weights_out(3)
    hidden_here()
    dense_layer()
    weights_first(3)
    weights_first(4)
    weights_out(4)
    normalize()
    tokens_first(0)
    weights_first(5)
    weights_first(6)
    tokens_first(1)
    tokens_first(2)
    tokens_second(0)
    weights_second(0)
    weights_second(1)
    weights_first(7)
    tokens_first(3)
    tokens_first(4)
    tokens_second(1)
    tokens_second(2)
    weights_second(2)
    weights_second(3)
    tokens_first(5)
    tokens_first(6)
    tokens_third(0)
    tokens_second(3)
    tokens_third(1)
    weights_second(4)
    tokens_second(4)
    tokens_third(2)
    tokens_first(7)
    weights_second(5)
    tokens_second(5)
    tokens_third(3)
    weights_second(6)
    tokens_second(6)
    tokens_third(4)
    weights_second(7)
    queries_out()
    queries_ring(0)
    pooled(0, 2)
    tokens_second(7)
    tokens_third(5)
    pooled(1, 2)
    tokens_third(6)
    tokens_third(7)
    queries_ring(1)
    queries_ring(2)
    pooled(2, 2)
    pooled(3, 2)
    queries_ring(3)
    queries_ring(4)
    weights_here()
    pooled_last()

    mx[x] = pool[x]
    own_bias.wait()
    for i in range(1, NX):
        fr = (x + i) % NX
        arrived(mx.at[fr], p_r.at[fr])
    peaks = jnp.concatenate(
        [
            mx[0, 0:8],
            mx[2, 0:8],
            jnp.maximum(mx[0, 8:16], mx[1, 8:16]),
            jnp.maximum(mx[2, 8:16], mx[3, 8:16]),
            mx[1, 0:8],
            mx[3, 0:8],
        ],
        axis=0,
    ) + biasv[...]
    reps = jnp.log1p(jnp.maximum(peaks, 0.0)).astype(BF16)
    rfull[enc] = reps

    def reps_ring(k):
        zz = zs[k]
        rows, sem = rfull.at[2 * zz + c], r_r.at[2 * zz + c]
        if k:
            arrived(rows, sem)
        ring_sends(k, rows, r_s, 0, sem)
        send(rows, rows, rs_s.at[k], sem, sibling)

    col = lax.broadcasted_iota(jnp.int32, (REPS, CW), 1)
    doubled = jnp.where(enc == NE - 1, NE * CW - COLS, 0)
    counted = jnp.where(col < doubled, 0.0, reps.astype(F32)).astype(BF16)
    own_q.wait()
    for i in range(1, NE):
        arrived(q_part((enc + i) % NE), q_r.at[(enc + i) % NE])
    sp[...] = lax.dot_general(
        counted, qall[...], (((1,), (1,)), ((), ())), preferred_element_type=F32
    )

    swapped = jnp.where(jnp.full((8, NQ), lens[0], jnp.int32) < 256, 1.0, 0.0)
    cbuf[0, 0:HALF, :] = sp[aligned(HALF * (1 - c), HALF), :]
    cbuf[0, HALF : HALF + 8, :] = swapped
    send(cbuf.at[0], cbuf.at[1], c_s.at[0], c_r.at[0], sibling)
    reps_ring(0)
    queries_ring(5)
    queries_ring(6)
    arrived(cbuf.at[1], c_r.at[0])
    xbuf[x] = sp[aligned(HALF * c, HALF), :] + cbuf[1, 0:HALF, :]
    theirs = cbuf[1, HALF : HALF + 8, :]
    for i in range(1, NX):
        send(xbuf.at[x], xbuf.at[x], x_s.at[i - 1], x_r.at[x], device(z, c, (x + i) % NX, y))
    reps_ring(1)
    reps_ring(2)
    queries_ring(7)
    for i in range(1, NX):
        arrived(xbuf.at[(x + i) % NX], x_r.at[(x + i) % NX])
    ybuf[y] = (xbuf[0] + xbuf[1]) + (xbuf[2] + xbuf[3])
    for i in range(1, NY):
        send(ybuf.at[y], ybuf.at[y], y_s.at[i - 1], y_r.at[y], device(z, c, x, (y + i) % NY))
    reps_ring(3)
    reps_ring(4)
    for i in range(1, NY):
        arrived(ybuf.at[(y + i) % NY], y_r.at[(y + i) % NY])
    row = lax.broadcasted_iota(jnp.int32, (8, NQ), 0)
    zbuf[z, 0:HALF, :] = (ybuf[0] + ybuf[1]) + (ybuf[2] + ybuf[3])
    zbuf[z, HALF : HALF + 8, :] = jnp.where((row // 4) == c, swapped, theirs)
    for i, away in enumerate((1, 7, 2, 6, 3, 5, 4)):
        send(zbuf.at[z], zbuf.at[z], z_s.at[i], z_r.at[z], device((z + away) % NZ, c, x, y))
    for k in (5, 6, 7):
        reps_ring(k)
    for i in range(1, NZ):
        arrived(zbuf.at[(z + i) % NZ], z_r.at[(z + i) % NZ])
    fin[aligned(HALF * c, HALF), :] = jnp.sum(zbuf[:, 0:HALF, :], axis=0)
    half = fin.at[aligned(HALF * c, HALF), :]
    send(half, half, c_s.at[1], c_r.at[1], sibling)
    flips = jnp.concatenate(
        [zbuf[zz, HALF + 4 * cc : HALF + 4 * cc + 1, :] for cc in range(2) for zz in range(NZ)],
        axis=0,
    )
    block = lax.broadcasted_iota(jnp.int32, (NE, NQ), 0)
    base = 3 * (2 * (block % 8) + block // 8)
    flip = jnp.where(flips > 0.5, 1, 0)
    passage = jnp.concatenate([base + flip, base + 1 - flip, base + 2], axis=0)
    is_positive = passage == positives[...]
    other = fin.at[aligned(HALF * (1 - c), HALF), :]
    arrived(other, c_r.at[1])

    scores = fin[...]
    peak = jnp.max(scores, axis=0, keepdims=True)
    log_total = jnp.log(jnp.sum(jnp.exp(scores - peak), axis=0, keepdims=True)) + peak
    picked = jnp.sum(jnp.where(is_positive, scores, 0.0), axis=0, keepdims=True)
    loss[...] = jnp.broadcast_to(
        jnp.sum(log_total - picked, axis=1, keepdims=True) * (1.0 / NQ), (8, NQ)
    )
    grad = jnp.exp(scores - log_total) - jnp.where(is_positive, 1.0, 0.0)
    sp[...] = grad
    gradT[...] = jnp.concatenate([grad, jnp.zeros((NQ - REPS, NQ), F32)], axis=0).T
    for_query = gradT[aligned(8 * enc, 8), 0:REPS].astype(BF16)
    block = 8 * c + z
    full_row, part_row = sp[pl.ds(block, 1), :], sp[pl.ds(16 + block, 1), :]
    last_row = sp[pl.ds(32 + block, 1), :]
    mine = swapped[0:1, :] > 0.5
    for_passage = jnp.concatenate(
        [
            jnp.where(mine, part_row, full_row),
            jnp.where(mine, full_row, part_row),
            last_row,
            jnp.zeros((5, NQ), F32),
        ],
        axis=0,
    ).astype(BF16)
    for zz in range(NZ):
        arrived(rfull.at[2 * zz + 1 - c], r_r.at[2 * zz + 1 - c])
        arrived(q_rows(zz, 1 - c), g_r.at[2 * zz + 1 - c])
    for ee in range(NE):
        skip = NE * CW - COLS if ee == NE - 1 else 0
        cols = slice(CW * ee, CW * (ee + 1) - skip)
        query_out[:, cols] = jnp.dot(for_query, rfull[ee], preferred_element_type=F32)[:, skip:]
        pass_out[:, cols] = jnp.dot(for_passage, qfull[:, cols], preferred_element_type=F32)[0:3]

    for i in range(1, NE):
        arrived(w_rows(x, enc), w_s.at[(enc + i) % NE])
        arrived(q_part(enc), q_s.at[i])
    for i in range(16):
        kind, yd, cd = hidden_dest(i)
        mine = jnp.logical_and(cd == c, jnp.logical_and(2 * c + kind == x, yd == y))

        @pl.when(jnp.logical_not(mine))
        def _():
            arrived(hsel.at[0], h_s.at[i])

    for k in range(7):
        arrived(dense_rows(z, c), d_s.at[k])
        arrived(rows_of(0, y), tz_s.at[k])
        arrived(q_rows(z, c), g_s.at[k])
        arrived(rfull.at[enc], r_s.at[k])
        arrived(zbuf.at[z], z_s.at[k])
    for k in range(NZ):
        arrived(dense_rows(z, c), ds_s.at[k])
        arrived(core_rows(0, c), ts_s.at[k])
        arrived(q_rows(z, c), gs_s.at[k])
        arrived(rfull.at[enc], rs_s.at[k])
    for k in range(24):
        arrived(rows_of(0, y), ty_s.at[k])
        arrived(w_pair(x, z), wx_s.at[k])
    for k in range(3):
        arrived(stat_all.at[y], st_s.at[k])
        arrived(mx.at[x], p_s.at[k])
        arrived(xbuf.at[x], x_s.at[k])
        arrived(ybuf.at[y], y_s.at[k])
    arrived(cbuf.at[0], c_s.at[0])
    arrived(half, c_s.at[1])


def call(lens, hid, dense, weight, queries, bias, positives):
    def dma(*n):
        return [pltpu.SemaphoreType.DMA((k,)) for k in n]

    hbm = pl.BlockSpec(memory_space=pltpu.HBM)
    vm = pl.BlockSpec(memory_space=pltpu.VMEM)
    return pl.pallas_call(
        kernel,
        out_shape=(
            jax.ShapeDtypeStruct((8, NQ), F32),
            jax.ShapeDtypeStruct((8, COLS), F32),
            jax.ShapeDtypeStruct((3, COLS), F32),
        ),
        in_specs=[pl.BlockSpec(memory_space=pltpu.SMEM), hbm, hbm, hbm, hbm, hbm, vm],
        out_specs=(vm, vm, vm),
        scratch_shapes=[
            pltpu.VMEM((64, 768), BF16),
            pltpu.VMEM((4, 64, 256), BF16),
            pltpu.VMEM((D, 256), BF16),
            pltpu.VMEM((256, D), F32),
            pltpu.VMEM((D, FW), BF16),
            pltpu.VMEM((ROWS, FW), F32),
            pltpu.VMEM((256, 128), F32),
            pltpu.VMEM((NY, 8, 256), F32),
            pltpu.VMEM((NZ, 2 * ROWS, D), BF16),
            pltpu.VMEM((NX, D, CW), BF16),
            pltpu.VMEM((NX, 16, CW), F32),
            pltpu.VMEM((NX, 16, CW), F32),
            pltpu.VMEM((NQ, CW), BF16),
            pltpu.VMEM((NQ, COLS), BF16),
            pltpu.VMEM((NE, REPS, CW), BF16),
            pltpu.VMEM((1, CW), F32),
            pltpu.VMEM((REPS, NQ), F32),
            pltpu.VMEM((2, HALF + 8, NQ), F32),
            pltpu.VMEM((NX, HALF, NQ), F32),
            pltpu.VMEM((NY, HALF, NQ), F32),
            pltpu.VMEM((NZ, HALF + 8, NQ), F32),
            pltpu.VMEM((REPS, NQ), F32),
            pltpu.VMEM((NQ, NQ), F32),
        ]
        + dma(6, 16, 16, 7, 16, 8, 16, 16, 16, 16, 3, 4)
        + dma(7, 24, 32, 8, 8, 24, 32, 7, 16, 8, 3, 4)
        + dma(7, 16, 8, 2, 2, 3, 4, 3, 4, 7, 8),
        compiler_params=pltpu.CompilerParams(
            collective_id=0, has_side_effects=True, vmem_limit_bytes=58 << 20
        ),
        name="splade_head",
    )(lens, hid, dense, weight, queries, bias, positives)


def per_device(hidden, dense_weight, head_weight, head_bias, lengths, queries, positives):
    loss, query_grad, passage_grad = call(
        lengths, hidden.T, dense_weight, head_weight, queries,
        head_bias.reshape(1, COLS), positives.reshape(1, NQ),
    )
    return loss[0, 0], query_grad, passage_grad


def solution(mesh):
    placed = (
        P("enc", ("vocab", "grp")),
        P("enc", None),
        P("enc", ("vocab", "grp")),
        P(("vocab", "grp")),
        P("enc"),
        P("enc", ("vocab", "grp")),
        P(),
    )
    return jax.shard_map(
        per_device,
        mesh=mesh,
        in_specs=placed,
        out_specs=(P(), P("enc", ("vocab", "grp")), P("enc", ("vocab", "grp"))),
        check_vma=False,
    )
```
